256 devices in a mesh: dp: 4 (over z_lo), expert: 64 (over z_hi, y, x, core).
Axes of the slice: x: 4, y: 4, z: 8 (z_hi: 2, z_lo: 4; z = z_hi * 4 + z_lo), core: 2. Of those that a mesh axis runs over, the one named last changes fastest.
Arguments:
- hidden: bfloat16 [262144, 768], P(('dp', 'expert')), may hold values from -6 to 6
- grad_out: bfloat16 [262144, 2048], P(('dp', 'expert')), may hold values from -0.19921875 to 0.19921875
- block_slot: int32 [256, 8], P(('dp', 'expert')), may hold values from 0 to 2, as said below
- block_count: int32 [256], P(('dp', 'expert')), may hold values from 2 to 8, as said below
- replica_expert: int32 [64], replicated, may hold values from 0 to 127, as said below
Outputs:
- grad_down: bfloat16 [128, 768, 2048], P('expert', None, 'dp')
The draws below stay inside these ranges and needn't reach their ends.
Inputs may be any that keep to these rules, and one draw needn't show every extreme that they name: `replica_expert`: Expert-axis index k is home to experts k * 2 to k * 2 + 1 and has one replica slot. The indices holding an expert homed at h are h alone, or h and (h + 32) mod 64, or h and (h + m * 16) mod 64 for m = 1, 2, 3; in every draw some expert homed at index 63 has such a set of four. `block_count`: some device has all 8 blocks live. `block_slot`: block 0 of every device belongs to the replica slot 2.
All inputs are finite; a program needn't handle non-finite values.
Results may differ from the reference program's by a relative error of at most 0.0065.
Values may be sent and summed in bfloat16 or wider, within the bound.
A program may use at most 128 MiB of HBM per device.

```python
import jax
import jax.numpy as jnp
from jax import lax

FF = 768
DW = 2048
EXP_DEV = 2
BLOCK = 128
BLOCKS = 8
HOSTS = 64
SHARDS = 4
EXPERTS = 128
TOKENS = 262144


def placement_table(key):
    quarter = HOSTS // 4
    base = jax.random.fold_in(key, 11)
    kind_key, home_key, local_key, four_key = jax.random.split(base, 4)
    groups = jnp.arange(quarter)
    kinds = jax.random.randint(kind_key, (quarter,), 0, 2)
    kinds = jnp.where((groups == 0) | (groups == quarter - 1), 1, kinds)
    home_pos = jax.random.randint(home_key, (quarter,), 0, 4)
    home_pos = jnp.where(groups == quarter - 1, 3, home_pos)
    local_pick = jax.random.randint(local_key, (quarter, 4), 0, EXP_DEV)
    four_pick = jax.random.randint(four_key, (quarter,), 0, EXP_DEV)
    column = jnp.arange(4)[None, :]
    group = groups[:, None]
    partner = (column + 2) % 4
    paired = (group + partner * quarter) * EXP_DEV + local_pick
    fourfold = (groups + home_pos * quarter) * EXP_DEV + four_pick
    use_four = (kinds[:, None] == 1) & (column != home_pos[:, None])
    chosen = jnp.where(use_four, fourfold[:, None], paired)
    return chosen.T.reshape(-1).astype(jnp.int32)


def draw_replica_expert(key, part):
    return placement_table(key)


def draw_block_slot(key, part):
    slot_key = jax.random.fold_in(key, 5)
    devices = SHARDS * HOSTS
    slots = jax.random.randint(slot_key, (devices, BLOCKS), 0, EXP_DEV + 1)
    first = jnp.arange(BLOCKS)[None, :] == 0
    return jnp.where(first, EXP_DEV, slots).astype(jnp.int32)


def draw_block_count(key, part):
    count_key = jax.random.fold_in(key, 7)
    devices = SHARDS * HOSTS
    counts = jax.random.randint(count_key, (devices,), max(1, BLOCKS // 4), BLOCKS + 1)
    counts = jnp.where(jnp.arange(devices) == 0, BLOCKS, counts)
    return counts.astype(jnp.int32)


def steps_of(own_key, shape, cuts, smallest, largest):
    gain, own = 1.0, jax.random.fold_in(own_key, 6)
    for dim, shards_of in cuts:
        steps = jnp.exp(jax.random.uniform(jax.random.fold_in(own, dim), (shards_of,), jnp.float32, smallest / len(cuts), largest / len(cuts)))
        gain = gain * jnp.repeat(steps, shape[dim] // shards_of).reshape([-1 if axis == dim else 1 for axis in range(len(shape))])
    return gain


def normal_values(rng, dims, spread, most, cuts=(), kind=jnp.bfloat16):
    entries = spread * jax.random.normal(rng, dims, jnp.float32)
    if cuts:
        entries = entries * steps_of(rng, dims, cuts, -0.22, 0.18)
    return jnp.clip(entries, -most, most).astype(kind)


def setup_inputs(seed: int = 0) -> dict:
    arg_keys = jax.random.split(jax.random.key(seed), 6)
    return {
        "hidden": normal_values(arg_keys[0], (TOKENS, FF), 1.0, 6.0, ((0, 256),)),
        "grad_out": normal_values(arg_keys[1], (TOKENS, DW), 0.03, 0.19921875, ((0, 256),)),
        "block_slot": draw_block_slot(jax.random.fold_in(arg_keys[5], 71), 0),
        "block_count": draw_block_count(jax.random.fold_in(arg_keys[5], 71), 0),
        "replica_expert": draw_replica_expert(jax.random.fold_in(arg_keys[5], 71), 0),
    }


def reference(hidden, grad_out, block_slot, block_count, replica_expert):
    total_blocks = hidden.shape[0] // BLOCK
    rows_in = hidden.reshape(total_blocks, BLOCK, FF)
    rows_out = grad_out.reshape(total_blocks, BLOCK, DW)
    position = jnp.arange(total_blocks, dtype=jnp.int32)
    device = position // BLOCKS
    holder = device % HOSTS
    slot_ids = block_slot.reshape(-1).astype(jnp.int32)
    owners = jnp.where(slot_ids < EXP_DEV, holder * EXP_DEV + slot_ids, replica_expert[holder]).astype(jnp.int32)
    block_live = (position % BLOCKS) < block_count[device]

    def add_block(totals, block_item):
        block_in, block_out, owner, live_flag = block_item

        def accumulate(current):
            product = jnp.dot(block_in.T, block_out, preferred_element_type=jnp.float32)
            return current.at[owner].add(product)

        def unchanged(current):
            return current

        return lax.cond(live_flag, accumulate, unchanged, totals), None

    totals = jnp.zeros((EXPERTS, FF, DW), jnp.float32)
    totals, _ = lax.scan(add_block, totals, (rows_in, rows_out, owners, block_live))
    return totals.astype(jnp.bfloat16)
```

```python
import jax
import jax.numpy as jnp
from jax import lax
from jax.sharding import PartitionSpec as P

EXP_DEV = 2
BLOCKS = 8


def slot_products(hidden, grad_out, slot_of, block_live):
    rows_per = hidden.shape[0] // slot_of.shape[0]
    results = []
    for slot in range(EXP_DEV + 1):
        chosen = (slot_of == slot) & block_live
        row_mask = jnp.repeat(chosen, rows_per).astype(hidden.dtype)
        masked = hidden * row_mask[:, None]
        results.append(
            lax.dot_general(
                masked, grad_out, (((0,), (0,)), ((), ())), preferred_element_type=jnp.float32
            ).astype(jnp.bfloat16)
        )
    return jnp.stack(results)


def swap(block, distance):
    n = lax.axis_size("expert")
    return lax.ppermute(block, "expert", [(i, i ^ distance) for i in range(n)])


def body(hidden, grad_out, block_slot, block_count, replica_expert):
    me = lax.axis_index("expert")
    half = lax.axis_size("expert") // 2
    quarter = half // 2
    live = jnp.arange(BLOCKS, dtype=jnp.int32) < block_count[0]
    mine = replica_expert[me]
    slots = block_slot[0]
    own = (slots == EXP_DEV) & (mine // EXP_DEV == me)
    slots = jnp.where(own, mine % EXP_DEV, slots)
    totals = slot_products(hidden, grad_out, slots, live)
    shares = lax.psum_scatter(totals, "dp", scatter_dimension=2, tiled=True)
    replica = shares[EXP_DEV]
    side = swap(replica, quarter)
    side_expert = replica_expert[me ^ quarter]
    across = me ^ half
    out = jnp.where(mine // EXP_DEV == across, replica.astype(jnp.float32), 0.0) + jnp.where(
        side_expert // EXP_DEV == across, side.astype(jnp.float32), 0.0
    )
    came = swap(out.astype(jnp.bfloat16), half)
    came_expert = replica_expert[across]
    home = []
    for slot in range(EXP_DEV):
        total = shares[slot].astype(jnp.float32)
        total += jnp.where(side_expert == me * EXP_DEV + slot, side.astype(jnp.float32), 0.0)
        total += jnp.where(came_expert == me * EXP_DEV + slot, came.astype(jnp.float32), 0.0)
        home.append(total.astype(jnp.bfloat16))
    return jnp.stack(home)


def solution(mesh):
    in_specs = (
        P(("dp", "expert"), None),
        P(("dp", "expert"), None),
        P(("dp", "expert"), None),
        P(("dp", "expert")),
        P(),
    )
    out_specs = P("expert", None, "dp")
    return jax.shard_map(body, mesh=mesh, in_specs=in_specs, out_specs=out_specs, check_vma=False)
```

```python
import functools

import jax
import jax.numpy as jnp
from jax import lax
from jax.experimental import pallas as pl
from jax.experimental.pallas import tpu as pltpu
from jax.sharding import PartitionSpec as P

EXP_DEV = 2
SUPER = 128
ROWS = 32
LAG = 2
OWN_LAG = 3
MESH = pl.DeviceIdType.MESH
F32 = jnp.float32
BF16 = jnp.bfloat16


def flag(condition):
    return jnp.where(condition, 1.0, 0.0).astype(F32)


def kernel(
    holders, slot_ref, count_ref, rep_ref, hid_ref, grad_ref, out_ref,
    lhs, home, rown, ra, rb, vs, vr, vx, hs, hr,
    y1_send, y2_send, v_send, h_send, ra_recv, rb_recv, vr_recv, vx_recv, hr_recv,
):
    lo = lax.axis_index("dp")
    me = lax.axis_index("expert")
    half = holders // 2
    quarter = holders // 4
    ystep = holders // 8
    hi = lax.div(me, half)
    ring = lax.rem(me, half)
    across = lax.rem(me + half, holders)
    side = hi * half + lax.rem(ring + quarter, half)
    upper = lax.div(lo, 2)
    outer = (lo == 0) | (lo == 3)
    inner = (lo == 1) | (lo == 2)

    tokens, ff = hid_ref.shape
    share = grad_ref.shape[1] // 4
    blocks = slot_ref.shape[0]
    block = tokens // blocks
    chunks = ff // ROWS
    per_super = SUPER // ROWS

    def y_target(n):
        step = ystep + lax.rem(n, 2) * (half - 2 * ystep)
        return hi * half + lax.rem(ring + step, half)

    barrier = pltpu.get_barrier_semaphore()
    up = (lax.rem(lo + 1, 4), lax.rem(me + lax.div(lo, 3) * half, holders))
    down = (lax.rem(lo + 3, 4), lax.rem(me + lax.div(3 - lo, 3) * half, holders))
    for target in (up, down, (lo, y_target(0)), (lo, y_target(1))):
        pl.semaphore_signal(barrier, inc=1, device_id=target, device_id_type=MESH)

    mine = rep_ref[me]
    beside = rep_ref[side]
    over = rep_ref[across]
    keep_own = flag(lax.div(mine, EXP_DEV) == across)
    keep_side = flag(lax.div(beside, EXP_DEV) == across)
    side_slot = [flag(beside == me * EXP_DEV + s) for s in range(EXP_DEV)]
    over_slot = [flag(over == me * EXP_DEV + s) for s in range(EXP_DEV)]
    home_here = lax.div(mine, EXP_DEV) == me
    weights = []
    for b in range(blocks):
        live = b < count_ref[0]
        slot = slot_ref[b]
        slot = jnp.where((slot == EXP_DEV) & home_here, lax.rem(mine, EXP_DEV), slot)
        weights.append([flag(live & (slot == s)) for s in range(EXP_DEV + 1)])

    def rows_of(c):
        return pl.ds(pl.multiple_of(c * ROWS, ROWS), ROWS)

    def outward(n):
        return n + upper * (3 - 2 * n)

    def swap_copy(c, n, src, dst, send_sem, recv_sem):
        j, rows = outward(n), rows_of(c)
        return pltpu.make_async_remote_copy(
            src_ref=src.at[j, rows], dst_ref=dst.at[j, rows],
            send_sem=send_sem, recv_sem=recv_sem.at[c, j],
            device_id=(lo, y_target(n)), device_id_type=MESH,
        )

    def first_swap(c, n):
        return swap_copy(c, n, rown, ra, y1_send, ra_recv)

    def second_swap(c, n):
        return swap_copy(c, n, ra, rb, y2_send, rb_recv)

    def to_outer(c, j):
        return pltpu.make_async_remote_copy(
            src_ref=vs.at[j, rows_of(c)], dst_ref=vr.at[j, rows_of(c)],
            send_sem=v_send, recv_sem=vr_recv.at[c, j],
            device_id=(3 * upper, me), device_id_type=MESH,
        )

    def to_across(c, j):
        return pltpu.make_async_remote_copy(
            src_ref=vs.at[j, rows_of(c)], dst_ref=vx.at[j, rows_of(c)],
            send_sem=v_send, recv_sem=vx_recv.at[c, j],
            device_id=(3 - lo, across), device_id_type=MESH,
        )

    def home_copy(c, j, place, target):
        return pltpu.make_async_remote_copy(
            src_ref=hs.at[j, :, rows_of(c)], dst_ref=hr.at[place, :, rows_of(c)],
            send_sem=h_send, recv_sem=hr_recv.at[c, place],
            device_id=(target, me), device_id_type=MESH,
        )

    def products(c):
        start = pl.multiple_of(c * ROWS, SUPER)
        lanes = pl.ds(start, SUPER)
        for b in range(blocks):
            turned = hid_ref[b * block:(b + 1) * block, lanes].astype(F32).T
            for s in range(EXP_DEV + 1):
                lhs[s * SUPER:(s + 1) * SUPER, b * block:(b + 1) * block] = (
                    turned * weights[b][s]
                ).astype(BF16)

        def one(n, carry):
            j = outward(n)
            columns = pl.ds(pl.multiple_of(j * share, share), share)
            made = jnp.dot(lhs[...], grad_ref[:, columns], preferred_element_type=F32)
            for s in range(EXP_DEV):
                home[j, s, lanes, :] = made[s * SUPER:(s + 1) * SUPER]
            rown[j, lanes, :] = made[EXP_DEV * SUPER:].astype(BF16)
            first_swap(c, n).start()
            return carry

        lax.fori_loop(0, 4, one, 0)

    def stage_a(c):
        @pl.when(lax.rem(c, per_super) == 0)
        def _():
            products(c)

        @pl.when(lax.rem(c, per_super) != 0)
        def _():
            def one(n, carry):
                first_swap(c, n).start()
                return carry

            lax.fori_loop(0, 4, one, 0)

    def stage_b(c):
        def one(n, carry):
            first_swap(c, n).wait_recv()
            second_swap(c, n).start()
            return carry

        lax.fori_loop(0, 4, one, 0)

    def stage_c(c):
        rows = rows_of(c)

        def one(n, carry):
            j = outward(n)
            second_swap(c, n).wait_recv()
            value = keep_own * rown[j, rows, :].astype(F32) + keep_side * rb[j, rows, :].astype(F32)

            @pl.when(inner)
            def _():
                vs[j, rows, :] = value.astype(BF16)
                to_outer(c, j).start()

            @pl.when(outer)
            def _():
                to_outer(c, j).wait_recv()
                vs[j, rows, :] = (value + vr[j, rows, :].astype(F32)).astype(BF16)
                to_across(c, j).start()

            return carry

        lax.fori_loop(0, 4, one, 0)

    def started(c, j, s):
        rows = rows_of(c)
        return home[j, s, rows, :] + side_slot[s] * rb[j, rows, :].astype(F32)

    def stage_d(c):
        rows = rows_of(c)

        def one(m, carry):
            last = lax.div(m, 2)
            j = (1 - last) * ((3 - m) - upper * (3 - 2 * m)) + last * (lo + 1 - 2 * lax.rem(lo, 2))

            @pl.when(outer)
            def _():
                to_across(c, j).wait_recv()
                for s in range(EXP_DEV):
                    hs[j, s, rows, :] = (
                        started(c, j, s) + over_slot[s] * vx[j, rows, :].astype(F32)
                    ).astype(BF16)

            @pl.when(inner)
            def _():
                home_copy(c, j, j, lax.rem(lo + 1, 4)).wait_recv()
                for s in range(EXP_DEV):
                    hs[j, s, rows, :] = (started(c, j, s) + hr[j, s, rows, :].astype(F32)).astype(BF16)

            @pl.when(j > lo)
            def _():
                home_copy(c, j, j, lax.rem(lo + 1, 4)).start()

            @pl.when(j == lo - 1)
            def _():
                home_copy(c, j, 4, lax.rem(lo + 3, 4)).start()

            @pl.when(j < lo - 1)
            def _():
                home_copy(c, j, j, lax.rem(lo + 3, 4)).start()

            return carry

        lax.fori_loop(0, 3, one, 0)

    def stage_e(c):
        rows = rows_of(c)

        @pl.when(outer)
        def _():
            place = 4 - lax.div(lo, 3)
            to_across(c, lo).wait_recv()
            home_copy(c, lo, place, lax.rem(lo + 1, 4)).wait_recv()
            for s in range(EXP_DEV):
                out_ref[s, rows, :] = (
                    started(c, lo, s)
                    + over_slot[s] * vx[lo, rows, :].astype(F32)
                    + hr[place, s, rows, :].astype(F32)
                ).astype(BF16)

        @pl.when(inner)
        def _():
            home_copy(c, lo, lo, lax.rem(lo + 1, 4)).wait_recv()
            home_copy(c, lo, 4, lax.rem(lo + 1, 4)).wait_recv()
            for s in range(EXP_DEV):
                out_ref[s, rows, :] = (
                    started(c, lo, s)
                    + hr[lo, s, rows, :].astype(F32)
                    + hr[4, s, rows, :].astype(F32)
                ).astype(BF16)

    def guarded(stage, c):
        @pl.when((c >= 0) & (c < chunks))
        def _():
            stage(c)

    pl.semaphore_wait(barrier, 4)
    extra = lax.div(3 - lo, 3) + lax.div(lo, 3)

    def tick(t, carry):
        guarded(stage_a, t)
        guarded(stage_b, t - 1)
        guarded(stage_c, t - 2 - extra)
        guarded(stage_d, t - 2 - LAG)
        guarded(stage_e, t - 2 - LAG - OWN_LAG)
        return carry

    lax.fori_loop(0, chunks + 2 + LAG + OWN_LAG, tick, 0)

    def drained(src, dst, sem):
        pltpu.make_async_remote_copy(
            src_ref=src, dst_ref=dst, send_sem=sem, recv_sem=vr_recv.at[0, 0],
            device_id=(lo, y_target(0)), device_id_type=MESH,
        ).wait_send()

    drained(rown, ra, y1_send)
    drained(ra, rb, y2_send)
    drained(vs, vr, v_send)
    drained(hs.at[0:3], hr.at[0:3], h_send)


def body(hidden, grad_out, block_slot, block_count, replica_expert):
    holders = lax.axis_size("expert")
    ff, width = hidden.shape[1], grad_out.shape[1]
    share = width // 4
    chunks = ff // ROWS
    column = (4, ff, share)
    dma = pltpu.SemaphoreType.DMA
    smem = pl.BlockSpec(memory_space=pltpu.SMEM)
    vmem = pl.BlockSpec(memory_space=pltpu.VMEM)
    return pl.pallas_call(
        functools.partial(kernel, holders),
        out_shape=jax.ShapeDtypeStruct((EXP_DEV, ff, share), BF16),
        in_specs=[smem, smem, smem, vmem, vmem],
        out_specs=vmem,
        scratch_shapes=[
            pltpu.VMEM(((EXP_DEV + 1) * SUPER, hidden.shape[0]), BF16),
            pltpu.VMEM((4, EXP_DEV, ff, share), F32),
            pltpu.VMEM(column, BF16),
            pltpu.VMEM(column, BF16),
            pltpu.VMEM(column, BF16),
            pltpu.VMEM(column, BF16),
            pltpu.VMEM(column, BF16),
            pltpu.VMEM(column, BF16),
            pltpu.VMEM((4, EXP_DEV, ff, share), BF16),
            pltpu.VMEM((5, EXP_DEV, ff, share), BF16),
            dma, dma, dma, dma,
            dma((chunks, 4)), dma((chunks, 4)), dma((chunks, 4)), dma((chunks, 4)), dma((chunks, 5)),
        ],
        compiler_params=pltpu.CompilerParams(
            collective_id=0, has_side_effects=True, vmem_limit_bytes=60 * 1024 * 1024
        ),
    )(block_slot[0], block_count, replica_expert, hidden, grad_out)


def solution(mesh):
    in_specs = (
        P(("dp", "expert"), None),
        P(("dp", "expert"), None),
        P(("dp", "expert"), None),
        P(("dp", "expert")),
        P(),
    )
    out_specs = P("expert", None, "dp")
    return jax.shard_map(body, mesh=mesh, in_specs=in_specs, out_specs=out_specs, check_vma=False)
```

```python
import functools

import jax
import jax.numpy as jnp
from jax import lax
from jax.experimental import pallas as pl
from jax.experimental.pallas import tpu as pltpu
from jax.sharding import PartitionSpec as P

EXP_DEV = 2
SUPER = 128
ROWS = 64
EARLY = 2
LAGS = {
    "T": (-1, -1),
    "A": (0, 0),
    "H": (1, 1),
    "C": (1, 1),
    "D": (1, 4),
    "G": (2, 6),
    "F": (4, 6),
    "E": (7, 11),
}
MESH = pl.DeviceIdType.MESH
F32 = jnp.float32
BF16 = jnp.bfloat16


def flag(condition):
    return jnp.where(condition, 1.0, 0.0).astype(F32)


def kernel(
    holders, slot_ref, count_ref, rep_ref, hid_hbm, grad_hbm, out_hbm,
    hid, grad, out, lhs, home, rown, rb, vs, vr, vx, hs, hr, zs, hz,
    in_sem, out_sem, y_send, v_send, h_send, z_send,
    rb_recv, vr_recv, vx_recv, hr_recv, z_recv,
):
    lo = lax.axis_index("dp")
    me = lax.axis_index("expert")
    half = holders // 2
    quarter = holders // 4
    hi = lax.div(me, half)
    across = lax.rem(me + half, holders)
    side = hi * half + lax.rem(lax.rem(me, half) + quarter, half)
    upper = lax.div(lo, 2)
    outer = (lo == 0) | (lo == 3)
    inner = (lo == 1) | (lo == 2)
    at_end = lax.div(3 - lo, 3) + lax.div(lo, 3)

    tokens, ff = hid.shape
    share = grad.shape[1] // 4
    blocks = slot_ref.shape[0]
    block = tokens // blocks
    chunks = ff // ROWS
    per_super = SUPER // ROWS

    barrier = pltpu.get_barrier_semaphore()
    up = (lax.rem(lo + 1, 4), lax.rem(me + lax.div(lo, 3) * half, holders))
    down = (lax.rem(lo + 3, 4), lax.rem(me + lax.div(3 - lo, 3) * half, holders))
    for target in (up, down, (lo, side)):
        pl.semaphore_signal(barrier, inc=1, device_id=target, device_id_type=MESH)

    def outward(n):
        return n + upper * (3 - 2 * n)

    def hidden_part(part):
        lanes = (slice(0, SUPER), slice(SUPER, ff))[part]
        return pltpu.make_async_copy(hid_hbm.at[:, lanes], hid.at[:, lanes], in_sem.at[4 + part])

    def columns_of(j):
        return pl.ds(pl.multiple_of(j * share, share), share)

    def grad_part(j):
        return pltpu.make_async_copy(
            grad_hbm.at[:, columns_of(j)], grad.at[:, columns_of(j)], in_sem.at[j]
        )

    hidden_part(0).start()
    for n in range(4):
        grad_part(outward(n)).start()
    if ff > SUPER:
        hidden_part(1).start()

    mine = rep_ref[me]
    beside = rep_ref[side]
    over = rep_ref[across]
    keep_own = flag(lax.div(mine, EXP_DEV) == across)
    keep_side = flag(lax.div(beside, EXP_DEV) == across)
    side_slot = [flag(beside == me * EXP_DEV + s) for s in range(EXP_DEV)]
    over_slot = [flag(over == me * EXP_DEV + s) for s in range(EXP_DEV)]
    late_slot = [jnp.maximum(side_slot[s], over_slot[s]) for s in range(EXP_DEV)]
    home_here = lax.div(mine, EXP_DEV) == me
    weights = []
    for b in range(blocks):
        live = b < count_ref[0]
        slot = slot_ref[b]
        slot = jnp.where((slot == EXP_DEV) & home_here, lax.rem(mine, EXP_DEV), slot)
        weights.append([flag(live & (slot == s)) for s in range(EXP_DEV + 1)])

    def rows_of(c):
        return pl.ds(pl.multiple_of(c * ROWS, ROWS), ROWS)

    def swap(c, j):
        return pltpu.make_async_remote_copy(
            src_ref=rown.at[j, rows_of(c)], dst_ref=rb.at[j, rows_of(c)],
            send_sem=y_send, recv_sem=rb_recv.at[c, j],
            device_id=(lo, side), device_id_type=MESH,
        )

    def to_outer(c, j):
        return pltpu.make_async_remote_copy(
            src_ref=vs.at[j, rows_of(c)], dst_ref=vr.at[j, rows_of(c)],
            send_sem=v_send, recv_sem=vr_recv.at[c, j],
            device_id=(3 * upper, me), device_id_type=MESH,
        )

    def to_across(c, j):
        return pltpu.make_async_remote_copy(
            src_ref=vs.at[j, rows_of(c)], dst_ref=vx.at[j, rows_of(c)],
            send_sem=v_send, recv_sem=vx_recv.at[c, j],
            device_id=(3 - lo, across), device_id_type=MESH,
        )

    def home_copy(c, j, place, target):
        return pltpu.make_async_remote_copy(
            src_ref=hs.at[j, :, rows_of(c)], dst_ref=hr.at[place, :, rows_of(c)],
            send_sem=h_send, recv_sem=hr_recv.at[c, place],
            device_id=(target, me), device_id_type=MESH,
        )

    def arrived(c, place):
        home_copy(c, 0, place, lax.rem(lo + 1, 4)).wait_recv()

    def late_copy(c, j):
        return pltpu.make_async_remote_copy(
            src_ref=zs.at[j, rows_of(c)], dst_ref=hz.at[j, rows_of(c)],
            send_sem=z_send, recv_sem=z_recv.at[c, j],
            device_id=(1 + upper, me), device_id_type=MESH,
        )

    def send_home(c, j):
        @pl.when(j > lo)
        def _():
            home_copy(c, j, j, lax.rem(lo + 1, 4)).start()

        @pl.when(j == lo - 1)
        def _():
            home_copy(c, j, 4, lax.rem(lo + 3, 4)).start()

        @pl.when(j < lo - 1)
        def _():
            home_copy(c, j, j, lax.rem(lo + 3, 4)).start()

    def side_of(c):
        return lax.rem(lax.div(c, per_super), 2)

    def turn(c):
        lanes = pl.ds(pl.multiple_of(c * ROWS, SUPER), SUPER)
        for b in range(blocks):
            turned = hid[b * block:(b + 1) * block, lanes].astype(F32).T
            for s in range(EXP_DEV + 1):
                lhs[side_of(c), s * SUPER:(s + 1) * SUPER, b * block:(b + 1) * block] = (
                    turned * weights[b][s]
                ).astype(BF16)

    def stage_t(c):
        @pl.when((c > 0) & (lax.rem(c, per_super) == 0))
        def _():
            @pl.when(c == per_super)
            def _():
                hidden_part(1).wait()

            turn(c)

    def stage_a(c):
        def one(n, carry):
            j = outward(n)

            @pl.when(lax.rem(c, per_super) == 0)
            def _():
                @pl.when(c == 0)
                def _():
                    grad_part(j).wait()

                lanes = pl.ds(pl.multiple_of(c * ROWS, SUPER), SUPER)
                made = jnp.dot(
                    lhs[side_of(c), EXP_DEV * SUPER:, :], grad[:, columns_of(j)],
                    preferred_element_type=F32,
                )
                rown[j, lanes, :] = made.astype(BF16)

            swap(c, j).start()
            return carry

        lax.fori_loop(0, 4, one, 0)

    def stage_h(c):
        @pl.when(lax.rem(c, per_super) == 0)
        def _():
            lanes = pl.ds(pl.multiple_of(c * ROWS, SUPER), SUPER)

            def one(n, carry):
                j = outward(3 - n)
                made = jnp.dot(
                    lhs[side_of(c), :EXP_DEV * SUPER, :], grad[:, columns_of(j)],
                    preferred_element_type=F32,
                )
                for s in range(EXP_DEV):
                    home[j, s, lanes, :] = made[s * SUPER:(s + 1) * SUPER]
                if EARLY:
                    @pl.when((c == 0) & outer & (n < 3))
                    def _():
                        for q in range(EARLY):
                            for s in range(EXP_DEV):
                                hs[j, s, rows_of(q), :] = home[j, s, rows_of(q), :].astype(BF16)
                            send_home(q, j)
                return carry

            lax.fori_loop(0, 4, one, 0)

    def stage_c(c):
        rows = rows_of(c)

        def one(n, carry):
            j = outward(n)
            swap(c, j).wait_recv()
            value = keep_own * rown[j, rows, :].astype(F32) + keep_side * rb[j, rows, :].astype(F32)

            @pl.when(inner)
            def _():
                vs[j, rows, :] = value.astype(BF16)
                to_outer(c, j).start()

            @pl.when(outer)
            def _():
                to_outer(c, j).wait_recv()
                vs[j, rows, :] = (value + vr[j, rows, :].astype(F32)).astype(BF16)
                to_across(c, j).start()

            return carry

        lax.fori_loop(0, 4, one, 0)

    def started(c, j, s):
        rows = rows_of(c)
        return home[j, s, rows, :] + side_slot[s] * rb[j, rows, :].astype(F32)

    def home_sum(c, m):
        rows = rows_of(c)
        j = (3 - m) - upper * (3 - 2 * m) if m < 2 else lo + 1 - 2 * lax.rem(lo, 2)

        @pl.when(outer)
        def _():
            to_across(c, j).wait_recv()

            @pl.when(c < EARLY)
            def _():
                zs[j, rows, :] = (
                    (side_slot[0] + side_slot[1]) * rb[j, rows, :].astype(F32)
                    + (over_slot[0] + over_slot[1]) * vx[j, rows, :].astype(F32)
                ).astype(BF16)
                late_copy(c, j).start()

            @pl.when(c >= EARLY)
            def _():
                for s in range(EXP_DEV):
                    hs[j, s, rows, :] = (
                        started(c, j, s) + over_slot[s] * vx[j, rows, :].astype(F32)
                    ).astype(BF16)
                send_home(c, j)

        @pl.when(inner)
        def _():
            arrived(c, j)

            def passed(extra):
                for s in range(EXP_DEV):
                    hs[j, s, rows, :] = (
                        started(c, j, s) + hr[j, s, rows, :].astype(F32) + extra(s)
                    ).astype(BF16)

            if m < 2 and EARLY:
                @pl.when(c < EARLY)
                def _():
                    late_copy(c, j).wait_recv()
                    passed(lambda s: late_slot[s] * hz[j, rows, :].astype(F32))

                @pl.when(c >= EARLY)
                def _():
                    passed(lambda s: 0.0)
            else:
                passed(lambda s: 0.0)
            send_home(c, j)

    def stage_d(c):
        home_sum(c, 0)

    def stage_g(c):
        home_sum(c, 1)

    def stage_f(c):
        home_sum(c, 2)

    def stage_e(c):
        rows = rows_of(c)

        @pl.when(outer)
        def _():
            place = 4 - lax.div(lo, 3)
            to_across(c, lo).wait_recv()
            arrived(c, place)
            for s in range(EXP_DEV):
                out[s, rows, :] = (
                    started(c, lo, s)
                    + over_slot[s] * vx[lo, rows, :].astype(F32)
                    + hr[place, s, rows, :].astype(F32)
                ).astype(BF16)

        @pl.when(inner)
        def _():
            arrived(c, lo)
            arrived(c, 4)

            def summed(extra):
                for s in range(EXP_DEV):
                    out[s, rows, :] = (
                        started(c, lo, s)
                        + hr[lo, s, rows, :].astype(F32)
                        + hr[4, s, rows, :].astype(F32)
                        + extra(s)
                    ).astype(BF16)

            if EARLY:
                @pl.when(c < EARLY)
                def _():
                    late_copy(c, lo).wait_recv()
                    summed(lambda s: late_slot[s] * hz[lo, rows, :].astype(F32))

                @pl.when(c >= EARLY)
                def _():
                    summed(lambda s: 0.0)
            else:
                summed(lambda s: 0.0)

        pltpu.make_async_copy(out.at[:, rows], out_hbm.at[:, rows], out_sem).start()

    hidden_part(0).wait()
    turn(0)
    pl.semaphore_wait(barrier, 3)

    def tick(t, carry):
        def guarded(stage, name):
            at, between = LAGS[name]
            c = t - between - at_end * (at - between)

            @pl.when((c >= 0) & (c < chunks))
            def _():
                stage(c)

        guarded(stage_f, "F")
        guarded(stage_a, "A")
        guarded(stage_h, "H")
        guarded(stage_c, "C")
        guarded(stage_g, "G")
        guarded(stage_t, "T")
        guarded(stage_d, "D")
        guarded(stage_e, "E")
        return carry

    lax.fori_loop(0, chunks + max(max(lags) for lags in LAGS.values()), tick, 0)

    def drained(src, dst, sem):
        pltpu.make_async_remote_copy(
            src_ref=src, dst_ref=dst, send_sem=sem, recv_sem=vr_recv.at[0, 0],
            device_id=(lo, side), device_id_type=MESH,
        ).wait_send()

    drained(rown, rb, y_send)
    drained(vs, vr, v_send)
    drained(hs.at[0:3], hr.at[0:3], h_send)
    if EARLY:
        @pl.when(outer)
        def _():
            drained(zs.at[0:3], hz.at[0:3], z_send)
    pltpu.make_async_copy(out, out_hbm, out_sem).wait()


def body(hidden, grad_out, block_slot, block_count, replica_expert):
    holders = lax.axis_size("expert")
    ff, width = hidden.shape[1], grad_out.shape[1]
    share = width // 4
    chunks = ff // ROWS
    column = (4, ff, share)
    early = (4, max(EARLY, 1) * ROWS, share)
    dma = pltpu.SemaphoreType.DMA
    smem = pl.BlockSpec(memory_space=pltpu.SMEM)
    hbm = pl.BlockSpec(memory_space=pl.ANY)
    return pl.pallas_call(
        functools.partial(kernel, holders),
        out_shape=jax.ShapeDtypeStruct((EXP_DEV, ff, share), BF16),
        in_specs=[smem, smem, smem, hbm, hbm],
        out_specs=hbm,
        scratch_shapes=[
            pltpu.VMEM(hidden.shape, BF16),
            pltpu.VMEM(grad_out.shape, BF16),
            pltpu.VMEM((EXP_DEV, ff, share), BF16),
            pltpu.VMEM((2, (EXP_DEV + 1) * SUPER, hidden.shape[0]), BF16),
            pltpu.VMEM((4, EXP_DEV, ff, share), F32),
            pltpu.VMEM(column, BF16),
            pltpu.VMEM(column, BF16),
            pltpu.VMEM(column, BF16),
            pltpu.VMEM(column, BF16),
            pltpu.VMEM(column, BF16),
            pltpu.VMEM((4, EXP_DEV, ff, share), BF16),
            pltpu.VMEM((5, EXP_DEV, ff, share), BF16),
            pltpu.VMEM(early, BF16),
            pltpu.VMEM(early, BF16),
            dma((6,)), dma, dma, dma, dma, dma,
            dma((chunks, 4)), dma((chunks, 4)), dma((chunks, 4)), dma((chunks, 5)),
            dma((max(EARLY, 1), 4)),
        ],
        compiler_params=pltpu.CompilerParams(
            collective_id=0, has_side_effects=True, vmem_limit_bytes=60 * 1024 * 1024
        ),
    )(block_slot[0], block_count, replica_expert, hidden, grad_out)


def solution(mesh):
    in_specs = (
        P(("dp", "expert"), None),
        P(("dp", "expert"), None),
        P(("dp", "expert"), None),
        P(("dp", "expert")),
        P(),
    )
    out_specs = P("expert", None, "dp")
    return jax.shard_map(body, mesh=mesh, in_specs=in_specs, out_specs=out_specs, check_vma=False)
```

```python
import functools

import jax
import jax.numpy as jnp
from jax import lax
from jax.experimental import pallas as pl
from jax.experimental.pallas import tpu as pltpu
from jax.sharding import PartitionSpec as P

EXP_DEV = 2
SUPER = 128
ROWS = 64
EARLY = 6
LAGS = {
    "T": (-1, -1),
    "A": (0, 0),
    "H": (1, 1),
    "C": (3, 1),
    "D": (3, 4),
    "G": (4, 6),
    "F": (6, 6),
    "E": (11, 10),
}
MESH = pl.DeviceIdType.MESH
F32 = jnp.float32
BF16 = jnp.bfloat16


def flag(condition):
    return jnp.where(condition, 1.0, 0.0).astype(F32)


def kernel(
    holders, slot_hbm, count_hbm, rep_hbm, hid_hbm, grad_hbm, out_hbm,
    slot_ref, count_ref, rep_ref, hid, grad, out, lhs, home, rown, rb, vs, vr, vx, hs, hr, zs, hz,
    int_sem, in_sem, out_sem, y_send, v_send, h_send, z_send,
    rb_recv, vr_recv, vx_recv, hr_recv, z_recv,
):
    lo = lax.axis_index("dp")
    me = lax.axis_index("expert")
    half = holders // 2
    quarter = holders // 4
    hi = lax.div(me, half)
    across = lax.rem(me + half, holders)
    side = hi * half + lax.rem(lax.rem(me, half) + quarter, half)
    upper = lax.div(lo, 2)
    outer = (lo == 0) | (lo == 3)
    inner = (lo == 1) | (lo == 2)
    at_end = lax.div(3 - lo, 3) + lax.div(lo, 3)

    tokens, ff = hid.shape
    share = grad.shape[1] // 4
    blocks = slot_ref.shape[0]
    block = tokens // blocks
    chunks = ff // ROWS
    per_super = SUPER // ROWS

    barrier = pltpu.get_barrier_semaphore()
    up = (lax.rem(lo + 1, 4), lax.rem(me + lax.div(lo, 3) * half, holders))
    down = (lax.rem(lo + 3, 4), lax.rem(me + lax.div(3 - lo, 3) * half, holders))
    for target in (up, down, (lo, side)):
        pl.semaphore_signal(barrier, inc=1, device_id=target, device_id_type=MESH)

    def outward(n):
        return n + upper * (3 - 2 * n)

    def hidden_part(part):
        lanes = (slice(0, SUPER), slice(SUPER, ff))[part]
        return pltpu.make_async_copy(hid_hbm.at[:, lanes], hid.at[:, lanes], in_sem.at[4 + part])

    def columns_of(j):
        return pl.ds(pl.multiple_of(j * share, share), share)

    def grad_part(j):
        return pltpu.make_async_copy(
            grad_hbm.at[:, columns_of(j)], grad.at[:, columns_of(j)], in_sem.at[j]
        )

    small = [
        pltpu.make_async_copy(src, dst, int_sem.at[k])
        for k, (src, dst) in enumerate(
            ((slot_hbm, slot_ref), (count_hbm, count_ref), (rep_hbm, rep_ref))
        )
    ]
    for copy in small:
        copy.start()
    hidden_part(0).start()
    for n in range(4):
        grad_part(outward(n + at_end * (3 - 2 * n) if EARLY else n)).start()
    if ff > SUPER:
        hidden_part(1).start()

    for copy in small:
        copy.wait()
    mine = rep_ref[me]
    beside = rep_ref[side]
    over = rep_ref[across]
    keep_own = flag(lax.div(mine, EXP_DEV) == across)
    keep_side = flag(lax.div(beside, EXP_DEV) == across)
    side_slot = [flag(beside == me * EXP_DEV + s) for s in range(EXP_DEV)]
    over_slot = [flag(over == me * EXP_DEV + s) for s in range(EXP_DEV)]
    late_slot = [jnp.maximum(side_slot[s], over_slot[s]) for s in range(EXP_DEV)]
    home_here = lax.div(mine, EXP_DEV) == me
    weights = []
    for b in range(blocks):
        live = b < count_ref[0]
        slot = slot_ref[b]
        slot = jnp.where((slot == EXP_DEV) & home_here, lax.rem(mine, EXP_DEV), slot)
        weights.append([flag(live & (slot == s)) for s in range(EXP_DEV + 1)])

    def rows_of(c):
        return pl.ds(pl.multiple_of(c * ROWS, ROWS), ROWS)

    def swap(c, j):
        return pltpu.make_async_remote_copy(
            src_ref=rown.at[j, rows_of(c)], dst_ref=rb.at[j, rows_of(c)],
            send_sem=y_send, recv_sem=rb_recv.at[c, j],
            device_id=(lo, side), device_id_type=MESH,
        )

    def to_outer(c, j):
        return pltpu.make_async_remote_copy(
            src_ref=vs.at[j, rows_of(c)], dst_ref=vr.at[j, rows_of(c)],
            send_sem=v_send, recv_sem=vr_recv.at[c, j],
            device_id=(3 * upper, me), device_id_type=MESH,
        )

    def to_across(c, j):
        return pltpu.make_async_remote_copy(
            src_ref=vs.at[j, rows_of(c)], dst_ref=vx.at[j, rows_of(c)],
            send_sem=v_send, recv_sem=vx_recv.at[c, j],
            device_id=(3 - lo, across), device_id_type=MESH,
        )

    def home_copy(c, j, place, target):
        return pltpu.make_async_remote_copy(
            src_ref=hs.at[j, :, rows_of(c)], dst_ref=hr.at[place, :, rows_of(c)],
            send_sem=h_send, recv_sem=hr_recv.at[c, place],
            device_id=(target, me), device_id_type=MESH,
        )

    def arrived(c, place):
        home_copy(c, 0, place, lax.rem(lo + 1, 4)).wait_recv()

    def late_copy(i):
        return pltpu.make_async_remote_copy(
            src_ref=zs.at[i], dst_ref=hz.at[i],
            send_sem=z_send, recv_sem=z_recv.at[i],
            device_id=(1 + upper, me), device_id_type=MESH,
        )

    def send_home(c, j):
        @pl.when(j > lo)
        def _():
            home_copy(c, j, j, lax.rem(lo + 1, 4)).start()

        @pl.when(j == lo - 1)
        def _():
            home_copy(c, j, 4, lax.rem(lo + 3, 4)).start()

        @pl.when(j < lo - 1)
        def _():
            home_copy(c, j, j, lax.rem(lo + 3, 4)).start()

    def side_of(c):
        return lax.rem(lax.div(c, per_super), 2)

    def turn(c):
        lanes = pl.ds(pl.multiple_of(c * ROWS, SUPER), SUPER)
        for b in range(blocks):
            turned = hid[b * block:(b + 1) * block, lanes].astype(F32).T
            for s in range(EXP_DEV + 1):
                lhs[side_of(c), s * SUPER:(s + 1) * SUPER, b * block:(b + 1) * block] = (
                    turned * weights[b][s]
                ).astype(BF16)

    def stage_t(c):
        @pl.when((c > 0) & (lax.rem(c, per_super) == 0))
        def _():
            @pl.when(c == per_super)
            def _():
                hidden_part(1).wait()

            turn(c)

    def stage_a(c):
        def one(n, carry):
            j = outward(n)

            @pl.when(lax.rem(c, per_super) == 0)
            def _():
                @pl.when((c == 0) & inner if EARLY else c == 0)
                def _():
                    grad_part(j).wait()

                lanes = pl.ds(pl.multiple_of(c * ROWS, SUPER), SUPER)
                made = jnp.dot(
                    lhs[side_of(c), EXP_DEV * SUPER:, :], grad[:, columns_of(j)],
                    preferred_element_type=F32,
                )
                rown[j, lanes, :] = made.astype(BF16)

            swap(c, j).start()
            return carry

        lax.fori_loop(0, 4, one, 0)

    def stage_h(c):
        @pl.when((lax.rem(c, per_super) == 0) & ((c > 0) | inner) if EARLY else lax.rem(c, per_super) == 0)
        def _():
            home_products(c)

    def home_products(c):
        lanes = pl.ds(pl.multiple_of(c * ROWS, SUPER), SUPER)

        def one(n, carry):
            j = outward(3 - n)
            if EARLY:
                @pl.when((c == 0) & outer)
                def _():
                    grad_part(j).wait()

            made = jnp.dot(
                lhs[side_of(c), :EXP_DEV * SUPER, :], grad[:, columns_of(j)],
                preferred_element_type=F32,
            )
            for s in range(EXP_DEV):
                home[j, s, lanes, :] = made[s * SUPER:(s + 1) * SUPER]
            if EARLY:
                @pl.when((c == 0) & outer & (n < 3))
                def _():
                    for q in range(pl.cdiv(EARLY, 3)):
                        @pl.when(3 * q + n < EARLY)
                        def _(q=q):
                            for s in range(EXP_DEV):
                                hs[j, s, rows_of(q), :] = home[j, s, rows_of(q), :].astype(BF16)
                            send_home(q, j)
            return carry

        lax.fori_loop(0, 4, one, 0)

    def stage_c(c):
        rows = rows_of(c)

        def one(n, carry):
            j = outward(n)
            swap(c, j).wait_recv()
            value = keep_own * rown[j, rows, :].astype(F32) + keep_side * rb[j, rows, :].astype(F32)

            @pl.when(inner)
            def _():
                vs[j, rows, :] = value.astype(BF16)
                to_outer(c, j).start()

            @pl.when(outer)
            def _():
                to_outer(c, j).wait_recv()
                vs[j, rows, :] = (value + vr[j, rows, :].astype(F32)).astype(BF16)
                to_across(c, j).start()

            return carry

        lax.fori_loop(0, 4, one, 0)

    def started(c, j, s):
        rows = rows_of(c)
        return home[j, s, rows, :] + side_slot[s] * rb[j, rows, :].astype(F32)

    def home_sum(c, m):
        rows = rows_of(c)
        j = (3 - m) - upper * (3 - 2 * m) if m < 2 else lo + 1 - 2 * lax.rem(lo, 2)

        @pl.when(outer)
        def _():
            to_across(c, j).wait_recv()

            @pl.when(3 * c + m < EARLY)
            def _():
                i = lax.rem(3 * c + m, max(EARLY, 1))
                zs[i] = (
                    (side_slot[0] + side_slot[1]) * rb[j, rows, :].astype(F32)
                    + (over_slot[0] + over_slot[1]) * vx[j, rows, :].astype(F32)
                ).astype(BF16)
                late_copy(i).start()

            @pl.when(3 * c + m >= EARLY)
            def _():
                for s in range(EXP_DEV):
                    hs[j, s, rows, :] = (
                        started(c, j, s) + over_slot[s] * vx[j, rows, :].astype(F32)
                    ).astype(BF16)
                send_home(c, j)

        @pl.when(inner)
        def _():
            arrived(c, j)

            def passed(extra):
                for s in range(EXP_DEV):
                    hs[j, s, rows, :] = (
                        started(c, j, s) + hr[j, s, rows, :].astype(F32) + extra(s)
                    ).astype(BF16)

            if m < 2 and EARLY:
                @pl.when(3 * c + m < EARLY)
                def _():
                    i = lax.rem(3 * c + m, EARLY)
                    late_copy(i).wait_recv()
                    passed(lambda s: late_slot[s] * hz[i].astype(F32))

                @pl.when(3 * c + m >= EARLY)
                def _():
                    passed(lambda s: 0.0)
            else:
                passed(lambda s: 0.0)
            send_home(c, j)

    def stage_d(c):
        home_sum(c, 0)

    def stage_g(c):
        home_sum(c, 1)

    def stage_f(c):
        home_sum(c, 2)

    def stage_e(c):
        rows = rows_of(c)

        @pl.when(outer)
        def _():
            place = 4 - lax.div(lo, 3)
            to_across(c, lo).wait_recv()
            arrived(c, place)
            for s in range(EXP_DEV):
                out[s, rows, :] = (
                    started(c, lo, s)
                    + over_slot[s] * vx[lo, rows, :].astype(F32)
                    + hr[place, s, rows, :].astype(F32)
                ).astype(BF16)

        @pl.when(inner)
        def _():
            arrived(c, lo)
            arrived(c, 4)

            def summed(extra):
                for s in range(EXP_DEV):
                    out[s, rows, :] = (
                        started(c, lo, s)
                        + hr[lo, s, rows, :].astype(F32)
                        + hr[4, s, rows, :].astype(F32)
                        + extra(s)
                    ).astype(BF16)

            if EARLY:
                @pl.when(3 * c + 2 < EARLY)
                def _():
                    i = lax.rem(3 * c + 2, EARLY)
                    late_copy(i).wait_recv()
                    summed(lambda s: late_slot[s] * hz[i].astype(F32))

                @pl.when(3 * c + 2 >= EARLY)
                def _():
                    summed(lambda s: 0.0)
            else:
                summed(lambda s: 0.0)

        pltpu.make_async_copy(out.at[:, rows], out_hbm.at[:, rows], out_sem).start()

    hidden_part(0).wait()
    turn(0)
    pl.semaphore_wait(barrier, 3)
    if EARLY:
        @pl.when(outer)
        def _():
            home_products(jnp.int32(0))

    def tick(t, carry):
        def guarded(stage, name):
            at, between = LAGS[name]
            c = t - between - at_end * (at - between)

            @pl.when((c >= 0) & (c < chunks))
            def _():
                stage(c)

        guarded(stage_h, "H")
        guarded(stage_a, "A")
        guarded(stage_f, "F")
        guarded(stage_g, "G")
        guarded(stage_c, "C")
        guarded(stage_e, "E")
        guarded(stage_d, "D")
        guarded(stage_t, "T")
        return carry

    lax.fori_loop(0, chunks + max(max(lags) for lags in LAGS.values()), tick, 0)

    def drained(src, dst, sem):
        pltpu.make_async_remote_copy(
            src_ref=src, dst_ref=dst, send_sem=sem, recv_sem=vr_recv.at[0, 0],
            device_id=(lo, side), device_id_type=MESH,
        ).wait_send()

    drained(rown, rb, y_send)
    drained(vs, vr, v_send)
    drained(hs.at[0:3], hr.at[0:3], h_send)
    if EARLY:
        @pl.when(outer)
        def _():
            drained(zs, hz, z_send)
    pltpu.make_async_copy(out, out_hbm, out_sem).wait()


def body(hidden, grad_out, block_slot, block_count, replica_expert):
    holders = lax.axis_size("expert")
    ff, width = hidden.shape[1], grad_out.shape[1]
    share = width // 4
    chunks = ff // ROWS
    column = (4, ff, share)
    early = (max(EARLY, 1), ROWS, share)
    dma = pltpu.SemaphoreType.DMA
    fixed = pl.BlockSpec(memory_space=pltpu.HBM)
    return pl.pallas_call(
        functools.partial(kernel, holders),
        out_shape=jax.ShapeDtypeStruct((EXP_DEV, ff, share), BF16),
        in_specs=[fixed] * 5,
        out_specs=pl.BlockSpec(memory_space=pl.ANY),
        scratch_shapes=[
            pltpu.SMEM((block_slot.shape[1],), jnp.int32),
            pltpu.SMEM(block_count.shape, jnp.int32),
            pltpu.SMEM(replica_expert.shape, jnp.int32),
            pltpu.VMEM(hidden.shape, BF16),
            pltpu.VMEM(grad_out.shape, BF16),
            pltpu.VMEM((EXP_DEV, ff, share), BF16),
            pltpu.VMEM((2, (EXP_DEV + 1) * SUPER, hidden.shape[0]), BF16),
            pltpu.VMEM((4, EXP_DEV, ff, share), F32),
            pltpu.VMEM(column, BF16),
            pltpu.VMEM(column, BF16),
            pltpu.VMEM(column, BF16),
            pltpu.VMEM(column, BF16),
            pltpu.VMEM(column, BF16),
            pltpu.VMEM((4, EXP_DEV, ff, share), BF16),
            pltpu.VMEM((5, EXP_DEV, ff, share), BF16),
            pltpu.VMEM(early, BF16),
            pltpu.VMEM(early, BF16),
            dma((3,)), dma((6,)), dma, dma, dma, dma, dma,
            dma((chunks, 4)), dma((chunks, 4)), dma((chunks, 4)), dma((chunks, 5)),
            dma((max(EARLY, 1),)),
        ],
        compiler_params=pltpu.CompilerParams(
            collective_id=0, has_side_effects=True, vmem_limit_bytes=52 * 1024 * 1024
        ),
    )(
        pltpu.with_memory_space_constraint(block_slot[0], pltpu.HBM), block_count,
        pltpu.with_memory_space_constraint(replica_expert, pltpu.HBM), hidden, grad_out,
    )


def solution(mesh):
    in_specs = (
        P(("dp", "expert"), None),
        P(("dp", "expert"), None),
        P(("dp", "expert"), None),
        P(("dp", "expert")),
        P(),
    )
    out_specs = P("expert", None, "dp")
    return jax.shard_map(body, mesh=mesh, in_specs=in_specs, out_specs=out_specs, check_vma=False)
```

```python
import functools

import jax
import jax.numpy as jnp
from jax import lax
from jax.experimental import pallas as pl
from jax.experimental.pallas import tpu as pltpu
from jax.sharding import PartitionSpec as P

EXP_DEV = 2
SUPER = 128
ROWS = 64
EARLY = 5
SWITCH = 8
LAGS = {
    "T": (-1, -1, 0, 0),
    "A": (0, 0, 0, 0),
    "H": (0, 0, 0, 0),
    "C": (1, 1, 0, 0),
    "D": (1, 5, 0, 0),
    "G": (2, 5, 0, 4),
    "F": (2, 9, 4, 0),
    "E": (14, 13, 4, 1),
}
MESH = pl.DeviceIdType.MESH
F32 = jnp.float32
BF16 = jnp.bfloat16


def flag(condition):
    return jnp.where(condition, 1.0, 0.0).astype(F32)


def kernel(
    holders, slot_hbm, count_hbm, rep_hbm, hid_hbm, grad_hbm, out_hbm,
    slot_ref, count_ref, rep_ref, hid, grad, out, lhs, home, rown, rb, vs, vr, vx, hs, hr, zs, hz,
    int_sem, in_sem, out_sem, y_send, v_send, h_send, z_send,
    rb_recv, vr_recv, vx_recv, hr_recv, z_recv,
):
    lo = lax.axis_index("dp")
    me = lax.axis_index("expert")
    half = holders // 2
    quarter = holders // 4
    hi = lax.div(me, half)
    across = lax.rem(me + half, holders)
    side = hi * half + lax.rem(lax.rem(me, half) + quarter, half)
    upper = lax.div(lo, 2)
    outer = (lo == 0) | (lo == 3)
    inner = (lo == 1) | (lo == 2)
    at_end = lax.div(3 - lo, 3) + lax.div(lo, 3)

    tokens, ff = hid.shape
    share = grad.shape[1] // 4
    blocks = slot_ref.shape[0]
    block = tokens // blocks
    chunks = ff // ROWS
    per_super = SUPER // ROWS

    barrier = pltpu.get_barrier_semaphore()
    up = (lax.rem(lo + 1, 4), lax.rem(me + lax.div(lo, 3) * half, holders))
    down = (lax.rem(lo + 3, 4), lax.rem(me + lax.div(3 - lo, 3) * half, holders))
    for target in (up, down, (lo, side)):
        pl.semaphore_signal(barrier, inc=1, device_id=target, device_id_type=MESH)

    def outward(n):
        return n + upper * (3 - 2 * n)

    def hidden_part(part):
        lanes = (slice(0, SUPER), slice(SUPER, ff))[part]
        return pltpu.make_async_copy(hid_hbm.at[:, lanes], hid.at[:, lanes], in_sem.at[4 + part])

    def columns_of(j):
        return pl.ds(pl.multiple_of(j * share, share), share)

    def grad_part(j):
        return pltpu.make_async_copy(
            grad_hbm.at[:, columns_of(j)], grad.at[:, columns_of(j)], in_sem.at[j]
        )

    small = [
        pltpu.make_async_copy(src, dst, int_sem.at[k])
        for k, (src, dst) in enumerate(
            ((slot_hbm, slot_ref), (count_hbm, count_ref), (rep_hbm, rep_ref))
        )
    ]
    for copy in small:
        copy.start()
    def needed(n):
        return outward(n + at_end * (3 - 2 * n) if EARLY else n)

    hidden_part(0).start()
    grad_part(needed(0)).start()

    for copy in small:
        copy.wait()
    mine = rep_ref[me]
    beside = rep_ref[side]
    over = rep_ref[across]
    keep_own = flag(lax.div(mine, EXP_DEV) == across)
    keep_side = flag(lax.div(beside, EXP_DEV) == across)
    side_slot = [flag(beside == me * EXP_DEV + s) for s in range(EXP_DEV)]
    over_slot = [flag(over == me * EXP_DEV + s) for s in range(EXP_DEV)]
    late_slot = [jnp.maximum(side_slot[s], over_slot[s]) for s in range(EXP_DEV)]
    home_here = lax.div(mine, EXP_DEV) == me
    weights = []
    for b in range(blocks):
        live = b < count_ref[0]
        slot = slot_ref[b]
        slot = jnp.where((slot == EXP_DEV) & home_here, lax.rem(mine, EXP_DEV), slot)
        weights.append([flag(live & (slot == s)) for s in range(EXP_DEV + 1)])

    def rows_of(c):
        return pl.ds(pl.multiple_of(c * ROWS, ROWS), ROWS)

    def swap(c, j):
        return pltpu.make_async_remote_copy(
            src_ref=rown.at[j, rows_of(c)], dst_ref=rb.at[j, rows_of(c)],
            send_sem=y_send, recv_sem=rb_recv.at[c, j],
            device_id=(lo, side), device_id_type=MESH,
        )

    def to_outer(c, j):
        return pltpu.make_async_remote_copy(
            src_ref=vs.at[j, rows_of(c)], dst_ref=vr.at[j, rows_of(c)],
            send_sem=v_send, recv_sem=vr_recv.at[c, j],
            device_id=(3 * upper, me), device_id_type=MESH,
        )

    def to_across(c, j):
        return pltpu.make_async_remote_copy(
            src_ref=vs.at[j, rows_of(c)], dst_ref=vx.at[j, rows_of(c)],
            send_sem=v_send, recv_sem=vx_recv.at[c, j],
            device_id=(3 - lo, across), device_id_type=MESH,
        )

    def home_copy(c, j, place, target):
        return pltpu.make_async_remote_copy(
            src_ref=hs.at[j, :, rows_of(c)], dst_ref=hr.at[place, :, rows_of(c)],
            send_sem=h_send, recv_sem=hr_recv.at[c, place],
            device_id=(target, me), device_id_type=MESH,
        )

    def arrived(c, place):
        home_copy(c, 0, place, lax.rem(lo + 1, 4)).wait_recv()

    def late_copy(i):
        return pltpu.make_async_remote_copy(
            src_ref=zs.at[i], dst_ref=hz.at[i],
            send_sem=z_send, recv_sem=z_recv.at[i],
            device_id=(1 + upper, me), device_id_type=MESH,
        )

    def send_home(c, j):
        @pl.when(j > lo)
        def _():
            home_copy(c, j, j, lax.rem(lo + 1, 4)).start()

        @pl.when(j == lo - 1)
        def _():
            home_copy(c, j, 4, lax.rem(lo + 3, 4)).start()

        @pl.when(j < lo - 1)
        def _():
            home_copy(c, j, j, lax.rem(lo + 3, 4)).start()

    def side_of(c):
        return lax.rem(lax.div(c, per_super), 2)

    def turn(c):
        lanes = pl.ds(pl.multiple_of(c * ROWS, SUPER), SUPER)
        for b in range(blocks):
            turned = hid[b * block:(b + 1) * block, lanes].astype(F32).T
            for s in range(EXP_DEV + 1):
                lhs[side_of(c), s * SUPER:(s + 1) * SUPER, b * block:(b + 1) * block] = (
                    turned * weights[b][s]
                ).astype(BF16)

    def stage_t(c):
        @pl.when((c > 0) & (lax.rem(c, per_super) == 0))
        def _():
            @pl.when(c == per_super)
            def _():
                hidden_part(1).wait()

            turn(c)

    def stage_a(c):
        def one(n, carry):
            j = outward(n)

            @pl.when(lax.rem(c, per_super) == 0)
            def _():
                @pl.when((c == 0) & inner if EARLY else c == 0)
                def _():
                    grad_part(j).wait()

                lanes = pl.ds(pl.multiple_of(c * ROWS, SUPER), SUPER)
                made = jnp.dot(
                    lhs[side_of(c), EXP_DEV * SUPER:, :], grad[:, columns_of(j)],
                    preferred_element_type=F32,
                )
                rown[j, lanes, :] = made.astype(BF16)

            swap(c, j).start()
            return carry

        lax.fori_loop(0, 4, one, 0)

    def stage_h(c):
        @pl.when((lax.rem(c, per_super) == 0) & ((c > 0) | inner) if EARLY else lax.rem(c, per_super) == 0)
        def _():
            home_products(c)

    def home_products(c):
        lanes = pl.ds(pl.multiple_of(c * ROWS, SUPER), SUPER)

        def one(n, carry):
            j = outward(3 - n)
            if EARLY:
                @pl.when((c == 0) & outer)
                def _():
                    grad_part(j).wait()

            made = jnp.dot(
                lhs[side_of(c), :EXP_DEV * SUPER, :], grad[:, columns_of(j)],
                preferred_element_type=F32,
            )
            for s in range(EXP_DEV):
                home[j, s, lanes, :] = made[s * SUPER:(s + 1) * SUPER]
            if EARLY:
                @pl.when((c == 0) & outer & (n < 3))
                def _():
                    for q in range(pl.cdiv(EARLY, 3)):
                        @pl.when(3 * q + n < EARLY)
                        def _(q=q):
                            for s in range(EXP_DEV):
                                hs[j, s, rows_of(q), :] = home[j, s, rows_of(q), :].astype(BF16)
                            send_home(q, j)
            return carry

        lax.fori_loop(0, 4, one, 0)

    def stage_c(c):
        rows = rows_of(c)

        def one(n, carry):
            j = outward(n)
            swap(c, j).wait_recv()
            value = keep_own * rown[j, rows, :].astype(F32) + keep_side * rb[j, rows, :].astype(F32)

            @pl.when(inner)
            def _():
                vs[j, rows, :] = value.astype(BF16)
                to_outer(c, j).start()

            @pl.when(outer)
            def _():
                to_outer(c, j).wait_recv()
                vs[j, rows, :] = (value + vr[j, rows, :].astype(F32)).astype(BF16)
                to_across(c, j).start()

            return carry

        lax.fori_loop(0, 4, one, 0)

    def started(c, j, s):
        rows = rows_of(c)
        return home[j, s, rows, :] + side_slot[s] * rb[j, rows, :].astype(F32)

    def home_sum(c, m):
        rows = rows_of(c)
        j = (3 - m) - upper * (3 - 2 * m) if m < 2 else lo + 1 - 2 * lax.rem(lo, 2)

        @pl.when(outer)
        def _():
            to_across(c, j).wait_recv()

            @pl.when(3 * c + m < EARLY)
            def _():
                i = lax.rem(3 * c + m, max(EARLY, 1))
                zs[i] = (
                    (side_slot[0] + side_slot[1]) * rb[j, rows, :].astype(F32)
                    + (over_slot[0] + over_slot[1]) * vx[j, rows, :].astype(F32)
                ).astype(BF16)
                late_copy(i).start()

            @pl.when(3 * c + m >= EARLY)
            def _():
                for s in range(EXP_DEV):
                    hs[j, s, rows, :] = (
                        started(c, j, s) + over_slot[s] * vx[j, rows, :].astype(F32)
                    ).astype(BF16)
                send_home(c, j)

        @pl.when(inner)
        def _():
            arrived(c, j)

            def passed(extra):
                for s in range(EXP_DEV):
                    hs[j, s, rows, :] = (
                        started(c, j, s) + hr[j, s, rows, :].astype(F32) + extra(s)
                    ).astype(BF16)

            if m < 2 and EARLY:
                @pl.when(3 * c + m < EARLY)
                def _():
                    i = lax.rem(3 * c + m, EARLY)
                    late_copy(i).wait_recv()
                    passed(lambda s: late_slot[s] * hz[i].astype(F32))

                @pl.when(3 * c + m >= EARLY)
                def _():
                    passed(lambda s: 0.0)
            else:
                passed(lambda s: 0.0)
            send_home(c, j)

    def stage_d(c):
        home_sum(c, 0)

    def stage_g(c):
        home_sum(c, 1)

    def stage_f(c):
        home_sum(c, 2)

    def stage_e(c):
        rows = rows_of(c)

        @pl.when(outer)
        def _():
            place = 4 - lax.div(lo, 3)
            to_across(c, lo).wait_recv()
            arrived(c, place)
            for s in range(EXP_DEV):
                out[s, rows, :] = (
                    started(c, lo, s)
                    + over_slot[s] * vx[lo, rows, :].astype(F32)
                    + hr[place, s, rows, :].astype(F32)
                ).astype(BF16)

        @pl.when(inner)
        def _():
            arrived(c, lo)
            arrived(c, 4)

            def summed(extra):
                for s in range(EXP_DEV):
                    out[s, rows, :] = (
                        started(c, lo, s)
                        + hr[lo, s, rows, :].astype(F32)
                        + hr[4, s, rows, :].astype(F32)
                        + extra(s)
                    ).astype(BF16)

            if EARLY:
                @pl.when(3 * c + 2 < EARLY)
                def _():
                    i = lax.rem(3 * c + 2, EARLY)
                    late_copy(i).wait_recv()
                    summed(lambda s: late_slot[s] * hz[i].astype(F32))

                @pl.when(3 * c + 2 >= EARLY)
                def _():
                    summed(lambda s: 0.0)
            else:
                summed(lambda s: 0.0)

        pltpu.make_async_copy(out.at[:, rows], out_hbm.at[:, rows], out_sem).start()

    hidden_part(0).wait()
    for n in range(1, 4):
        grad_part(needed(n)).start()
    if ff > SUPER:
        hidden_part(1).start()
    turn(0)
    pl.semaphore_wait(barrier, 3)
    if EARLY:
        @pl.when(outer)
        def _():
            home_products(jnp.int32(0))

    def tick(first, t, carry):
        def guarded(stage, name):
            at, between, at_more, between_more = LAGS[name]
            lag = between + at_end * (at - between)
            more = between_more + at_end * (at_more - between_more)
            c = t - lag if first else t - lag - more
            start = 0 if first else SWITCH - lag

            @pl.when((c >= 0) & (c >= start) & (c < chunks))
            def _():
                stage(c)

        guarded(stage_a, "A")
        guarded(stage_g, "G")
        guarded(stage_f, "F")
        guarded(stage_e, "E")
        guarded(stage_c, "C")
        guarded(stage_d, "D")
        guarded(stage_t, "T")
        guarded(stage_h, "H")
        return carry

    ticks = chunks + max(max(lags[0] + lags[2], lags[1] + lags[3]) for lags in LAGS.values())
    lax.fori_loop(0, SWITCH, functools.partial(tick, True), 0)
    lax.fori_loop(SWITCH, ticks, functools.partial(tick, False), 0)

    def drained(src, dst, sem):
        pltpu.make_async_remote_copy(
            src_ref=src, dst_ref=dst, send_sem=sem, recv_sem=vr_recv.at[0, 0],
            device_id=(lo, side), device_id_type=MESH,
        ).wait_send()

    drained(rown, rb, y_send)
    drained(vs, vr, v_send)
    drained(hs.at[0:3], hr.at[0:3], h_send)
    if EARLY:
        @pl.when(outer)
        def _():
            drained(zs, hz, z_send)
    pltpu.make_async_copy(out, out_hbm, out_sem).wait()


def body(hidden, grad_out, block_slot, block_count, replica_expert):
    holders = lax.axis_size("expert")
    ff, width = hidden.shape[1], grad_out.shape[1]
    share = width // 4
    chunks = ff // ROWS
    column = (4, ff, share)
    early = (max(EARLY, 1), ROWS, share)
    dma = pltpu.SemaphoreType.DMA
    fixed = pl.BlockSpec(memory_space=pltpu.HBM)
    return pl.pallas_call(
        functools.partial(kernel, holders),
        out_shape=jax.ShapeDtypeStruct((EXP_DEV, ff, share), BF16),
        in_specs=[fixed] * 5,
        out_specs=pl.BlockSpec(memory_space=pl.ANY),
        scratch_shapes=[
            pltpu.SMEM((block_slot.shape[1],), jnp.int32),
            pltpu.SMEM(block_count.shape, jnp.int32),
            pltpu.SMEM(replica_expert.shape, jnp.int32),
            pltpu.VMEM(hidden.shape, BF16),
            pltpu.VMEM(grad_out.shape, BF16),
            pltpu.VMEM((EXP_DEV, ff, share), BF16),
            pltpu.VMEM((2, (EXP_DEV + 1) * SUPER, hidden.shape[0]), BF16),
            pltpu.VMEM((4, EXP_DEV, ff, share), F32),
            pltpu.VMEM(column, BF16),
            pltpu.VMEM(column, BF16),
            pltpu.VMEM(column, BF16),
            pltpu.VMEM(column, BF16),
            pltpu.VMEM(column, BF16),
            pltpu.VMEM((4, EXP_DEV, ff, share), BF16),
            pltpu.VMEM((5, EXP_DEV, ff, share), BF16),
            pltpu.VMEM(early, BF16),
            pltpu.VMEM(early, BF16),
            dma((3,)), dma((6,)), dma, dma, dma, dma, dma,
            dma((chunks, 4)), dma((chunks, 4)), dma((chunks, 4)), dma((chunks, 5)),
            dma((max(EARLY, 1),)),
        ],
        compiler_params=pltpu.CompilerParams(
            collective_id=0, has_side_effects=True, vmem_limit_bytes=52 * 1024 * 1024
        ),
    )(
        pltpu.with_memory_space_constraint(block_slot[0], pltpu.HBM), block_count,
        pltpu.with_memory_space_constraint(replica_expert, pltpu.HBM), hidden, grad_out,
    )


def solution(mesh):
    in_specs = (
        P(("dp", "expert"), None),
        P(("dp", "expert"), None),
        P(("dp", "expert"), None),
        P(("dp", "expert")),
        P(),
    )
    out_specs = P("expert", None, "dp")
    return jax.shard_map(body, mesh=mesh, in_specs=in_specs, out_specs=out_specs, check_vma=False)
```

```python
import functools

import jax
import jax.numpy as jnp
from jax import lax
from jax.experimental import pallas as pl
from jax.experimental.pallas import tpu as pltpu
from jax.sharding import PartitionSpec as P

EXP_DEV = 2
SUPER = 128
ROWS = 64
EARLY = 5
SWITCH = 8
LAGS = {
    "T": (-1, -1, 0, 0),
    "A": (0, 0, 0, 0),
    "H": (0, 0, 0, 0),
    "C": (1, 1, 0, 0),
    "D": (1, 5, 0, 0),
    "G": (2, 5, 0, 3),
    "F": (2, 8, 3, 0),
    "E": (12, 12, 2, 1),
}
MESH = pl.DeviceIdType.MESH
F32 = jnp.float32
BF16 = jnp.bfloat16


def flag(condition):
    return jnp.where(condition, 1.0, 0.0).astype(F32)


def kernel(
    holders, slot_hbm, count_hbm, rep_hbm, hid_hbm, grad_hbm, out_hbm,
    slot_ref, count_ref, rep_ref, hid, grad, out, lhs, home, rown, rb, vs, vr, vx, hs, hr, zs, hz,
    int_sem, in_sem, out_sem, y_send, v_send, h_send, z_send,
    rb_recv, vr_recv, vx_recv, hr_recv, z_recv,
):
    lo = lax.axis_index("dp")
    me = lax.axis_index("expert")
    half = holders // 2
    quarter = holders // 4
    hi = lax.div(me, half)
    across = lax.rem(me + half, holders)
    side = hi * half + lax.rem(lax.rem(me, half) + quarter, half)
    upper = lax.div(lo, 2)
    outer = (lo == 0) | (lo == 3)
    inner = (lo == 1) | (lo == 2)
    at_end = lax.div(3 - lo, 3) + lax.div(lo, 3)

    tokens, ff = hid.shape
    share = grad.shape[1] // 4
    blocks = slot_ref.shape[0]
    block = tokens // blocks
    chunks = ff // ROWS
    per_super = SUPER // ROWS

    barrier = pltpu.get_barrier_semaphore()
    up = (lax.rem(lo + 1, 4), lax.rem(me + lax.div(lo, 3) * half, holders))
    down = (lax.rem(lo + 3, 4), lax.rem(me + lax.div(3 - lo, 3) * half, holders))
    for target in (up, down, (lo, side)):
        pl.semaphore_signal(barrier, inc=1, device_id=target, device_id_type=MESH)

    def outward(n):
        return n + upper * (3 - 2 * n)

    def hidden_part(part):
        lanes = (slice(0, SUPER), slice(SUPER, ff))[part]
        return pltpu.make_async_copy(hid_hbm.at[:, lanes], hid.at[:, lanes], in_sem.at[4 + part])

    def columns_of(j):
        return pl.ds(pl.multiple_of(j * share, share), share)

    def grad_part(j):
        return pltpu.make_async_copy(
            grad_hbm.at[:, columns_of(j)], grad.at[:, columns_of(j)], in_sem.at[j]
        )

    small = [
        pltpu.make_async_copy(src, dst, int_sem.at[k])
        for k, (src, dst) in enumerate(
            ((slot_hbm, slot_ref), (count_hbm, count_ref), (rep_hbm, rep_ref))
        )
    ]
    for copy in small:
        copy.start()
    hidden_part(0).start()
    for n in range(4):
        grad_part(outward(n + at_end * (3 - 2 * n) if EARLY else n)).start()
    if ff > SUPER:
        hidden_part(1).start()

    for copy in small:
        copy.wait()
    mine = rep_ref[me]
    beside = rep_ref[side]
    over = rep_ref[across]
    keep_own = flag(lax.div(mine, EXP_DEV) == across)
    keep_side = flag(lax.div(beside, EXP_DEV) == across)
    side_slot = [flag(beside == me * EXP_DEV + s) for s in range(EXP_DEV)]
    over_slot = [flag(over == me * EXP_DEV + s) for s in range(EXP_DEV)]
    late_slot = [jnp.maximum(side_slot[s], over_slot[s]) for s in range(EXP_DEV)]
    home_here = lax.div(mine, EXP_DEV) == me
    weights = []
    for b in range(blocks):
        live = b < count_ref[0]
        slot = slot_ref[b]
        slot = jnp.where((slot == EXP_DEV) & home_here, lax.rem(mine, EXP_DEV), slot)
        weights.append([flag(live & (slot == s)) for s in range(EXP_DEV + 1)])

    def rows_of(c):
        return pl.ds(pl.multiple_of(c * ROWS, ROWS), ROWS)

    def swap(c, j):
        return pltpu.make_async_remote_copy(
            src_ref=rown.at[j, rows_of(c)], dst_ref=rb.at[j, rows_of(c)],
            send_sem=y_send, recv_sem=rb_recv.at[c, j],
            device_id=(lo, side), device_id_type=MESH,
        )

    def to_outer(c, j):
        return pltpu.make_async_remote_copy(
            src_ref=vs.at[j, rows_of(c)], dst_ref=vr.at[j, rows_of(c)],
            send_sem=v_send, recv_sem=vr_recv.at[c, j],
            device_id=(3 * upper, me), device_id_type=MESH,
        )

    def to_across(c, j):
        return pltpu.make_async_remote_copy(
            src_ref=vs.at[j, rows_of(c)], dst_ref=vx.at[j, rows_of(c)],
            send_sem=v_send, recv_sem=vx_recv.at[c, j],
            device_id=(3 - lo, across), device_id_type=MESH,
        )

    def home_copy(c, j, place, target):
        return pltpu.make_async_remote_copy(
            src_ref=hs.at[j, :, rows_of(c)], dst_ref=hr.at[place, :, rows_of(c)],
            send_sem=h_send, recv_sem=hr_recv.at[c, place],
            device_id=(target, me), device_id_type=MESH,
        )

    def arrived(c, place):
        home_copy(c, 0, place, lax.rem(lo + 1, 4)).wait_recv()

    def late_copy(i):
        return pltpu.make_async_remote_copy(
            src_ref=zs.at[i], dst_ref=hz.at[i],
            send_sem=z_send, recv_sem=z_recv.at[i],
            device_id=(1 + upper, me), device_id_type=MESH,
        )

    def send_home(c, j):
        @pl.when(j > lo)
        def _():
            home_copy(c, j, j, lax.rem(lo + 1, 4)).start()

        @pl.when(j == lo - 1)
        def _():
            home_copy(c, j, 4, lax.rem(lo + 3, 4)).start()

        @pl.when(j < lo - 1)
        def _():
            home_copy(c, j, j, lax.rem(lo + 3, 4)).start()

    def side_of(c):
        return lax.rem(lax.div(c, per_super), 2)

    def turn(c):
        lanes = pl.ds(pl.multiple_of(c * ROWS, SUPER), SUPER)
        for b in range(blocks):
            turned = hid[b * block:(b + 1) * block, lanes].astype(F32).T
            for s in range(EXP_DEV + 1):
                lhs[side_of(c), s * SUPER:(s + 1) * SUPER, b * block:(b + 1) * block] = (
                    turned * weights[b][s]
                ).astype(BF16)

    def stage_t(c):
        @pl.when((c > 0) & (lax.rem(c, per_super) == 0))
        def _():
            @pl.when(c == per_super)
            def _():
                hidden_part(1).wait()

            turn(c)

    def stage_a(c):
        def one(n, carry):
            j = outward(n)

            @pl.when(lax.rem(c, per_super) == 0)
            def _():
                @pl.when((c == 0) & inner if EARLY else c == 0)
                def _():
                    grad_part(j).wait()

                lanes = pl.ds(pl.multiple_of(c * ROWS, SUPER), SUPER)
                made = jnp.dot(
                    lhs[side_of(c), EXP_DEV * SUPER:, :], grad[:, columns_of(j)],
                    preferred_element_type=F32,
                )
                rown[j, lanes, :] = made.astype(BF16)

            swap(c, j).start()
            return carry

        lax.fori_loop(0, 4, one, 0)

    def stage_h(c):
        @pl.when((lax.rem(c, per_super) == 0) & ((c > 0) | inner) if EARLY else lax.rem(c, per_super) == 0)
        def _():
            home_products(c)

    def home_products(c):
        lanes = pl.ds(pl.multiple_of(c * ROWS, SUPER), SUPER)

        def one(n, carry):
            j = outward(3 - n)
            if EARLY:
                @pl.when((c == 0) & outer)
                def _():
                    grad_part(j).wait()

            made = jnp.dot(
                lhs[side_of(c), :EXP_DEV * SUPER, :], grad[:, columns_of(j)],
                preferred_element_type=F32,
            )
            for s in range(EXP_DEV):
                home[j, s, lanes, :] = made[s * SUPER:(s + 1) * SUPER]
            if EARLY:
                @pl.when((c == 0) & outer & (n < 3))
                def _():
                    for q in range(pl.cdiv(EARLY, 3)):
                        @pl.when(3 * q + n < EARLY)
                        def _(q=q):
                            for s in range(EXP_DEV):
                                hs[j, s, rows_of(q), :] = home[j, s, rows_of(q), :].astype(BF16)
                            send_home(q, j)
            return carry

        lax.fori_loop(0, 4, one, 0)

    def stage_c(c):
        rows = rows_of(c)

        def one(n, carry):
            j = outward(n)
            swap(c, j).wait_recv()
            value = keep_own * rown[j, rows, :].astype(F32) + keep_side * rb[j, rows, :].astype(F32)

            @pl.when(inner)
            def _():
                vs[j, rows, :] = value.astype(BF16)
                to_outer(c, j).start()

            @pl.when(outer)
            def _():
                to_outer(c, j).wait_recv()
                vs[j, rows, :] = (value + vr[j, rows, :].astype(F32)).astype(BF16)
                to_across(c, j).start()

            return carry

        lax.fori_loop(0, 4, one, 0)

    def started(c, j, s):
        rows = rows_of(c)
        return home[j, s, rows, :] + side_slot[s] * rb[j, rows, :].astype(F32)

    def home_sum(c, m):
        rows = rows_of(c)
        j = (3 - m) - upper * (3 - 2 * m) if m < 2 else lo + 1 - 2 * lax.rem(lo, 2)

        @pl.when(outer)
        def _():
            to_across(c, j).wait_recv()

            @pl.when(3 * c + m < EARLY)
            def _():
                i = lax.rem(3 * c + m, max(EARLY, 1))
                zs[i] = (
                    (side_slot[0] + side_slot[1]) * rb[j, rows, :].astype(F32)
                    + (over_slot[0] + over_slot[1]) * vx[j, rows, :].astype(F32)
                ).astype(BF16)
                late_copy(i).start()

            @pl.when(3 * c + m >= EARLY)
            def _():
                for s in range(EXP_DEV):
                    hs[j, s, rows, :] = (
                        started(c, j, s) + over_slot[s] * vx[j, rows, :].astype(F32)
                    ).astype(BF16)
                send_home(c, j)

        @pl.when(inner)
        def _():
            arrived(c, j)

            def passed(extra):
                for s in range(EXP_DEV):
                    hs[j, s, rows, :] = (
                        started(c, j, s) + hr[j, s, rows, :].astype(F32) + extra(s)
                    ).astype(BF16)

            if m < 2 and EARLY:
                @pl.when(3 * c + m < EARLY)
                def _():
                    i = lax.rem(3 * c + m, EARLY)
                    late_copy(i).wait_recv()
                    passed(lambda s: late_slot[s] * hz[i].astype(F32))

                @pl.when(3 * c + m >= EARLY)
                def _():
                    passed(lambda s: 0.0)
            else:
                passed(lambda s: 0.0)
            send_home(c, j)

    def stage_d(c):
        home_sum(c, 0)

    def stage_g(c):
        home_sum(c, 1)

    def stage_f(c):
        home_sum(c, 2)

    def stage_e(c):
        rows = rows_of(c)

        @pl.when(outer)
        def _():
            place = 4 - lax.div(lo, 3)
            to_across(c, lo).wait_recv()
            arrived(c, place)
            for s in range(EXP_DEV):
                out[s, rows, :] = (
                    started(c, lo, s)
                    + over_slot[s] * vx[lo, rows, :].astype(F32)
                    + hr[place, s, rows, :].astype(F32)
                ).astype(BF16)

        @pl.when(inner)
        def _():
            arrived(c, lo)
            arrived(c, 4)

            def summed(extra):
                for s in range(EXP_DEV):
                    out[s, rows, :] = (
                        started(c, lo, s)
                        + hr[lo, s, rows, :].astype(F32)
                        + hr[4, s, rows, :].astype(F32)
                        + extra(s)
                    ).astype(BF16)

            if EARLY:
                @pl.when(3 * c + 2 < EARLY)
                def _():
                    i = lax.rem(3 * c + 2, EARLY)
                    late_copy(i).wait_recv()
                    summed(lambda s: late_slot[s] * hz[i].astype(F32))

                @pl.when(3 * c + 2 >= EARLY)
                def _():
                    summed(lambda s: 0.0)
            else:
                summed(lambda s: 0.0)

        pltpu.make_async_copy(out.at[:, rows], out_hbm.at[:, rows], out_sem).start()

    hidden_part(0).wait()
    turn(0)
    pl.semaphore_wait(barrier, 3)
    if EARLY:
        @pl.when(outer)
        def _():
            home_products(jnp.int32(0))

    def tick(first, t, carry):
        def guarded(stage, name):
            at, between, at_more, between_more = LAGS[name]
            lag = between + at_end * (at - between)
            more = between_more + at_end * (at_more - between_more)
            c = t - lag if first else t - lag - more
            start = 0 if first else SWITCH - lag

            @pl.when((c >= 0) & (c >= start) & (c < chunks))
            def _():
                stage(c)

        guarded(stage_a, "A")
        guarded(stage_g, "G")
        guarded(stage_f, "F")
        guarded(stage_e, "E")
        guarded(stage_c, "C")
        guarded(stage_d, "D")
        guarded(stage_t, "T")
        guarded(stage_h, "H")
        return carry

    ticks = chunks + max(max(lags[0] + lags[2], lags[1] + lags[3]) for lags in LAGS.values())
    lax.fori_loop(0, SWITCH, functools.partial(tick, True), 0)
    lax.fori_loop(SWITCH, ticks, functools.partial(tick, False), 0)

    def drained(src, dst, sem):
        pltpu.make_async_remote_copy(
            src_ref=src, dst_ref=dst, send_sem=sem, recv_sem=vr_recv.at[0, 0],
            device_id=(lo, side), device_id_type=MESH,
        ).wait_send()

    drained(rown, rb, y_send)
    drained(vs, vr, v_send)
    drained(hs.at[0:3], hr.at[0:3], h_send)
    if EARLY:
        @pl.when(outer)
        def _():
            drained(zs, hz, z_send)
    pltpu.make_async_copy(out, out_hbm, out_sem).wait()


def body(hidden, grad_out, block_slot, block_count, replica_expert):
    holders = lax.axis_size("expert")
    ff, width = hidden.shape[1], grad_out.shape[1]
    share = width // 4
    chunks = ff // ROWS
    column = (4, ff, share)
    early = (max(EARLY, 1), ROWS, share)
    dma = pltpu.SemaphoreType.DMA
    fixed = pl.BlockSpec(memory_space=pltpu.HBM)
    return pl.pallas_call(
        functools.partial(kernel, holders),
        out_shape=jax.ShapeDtypeStruct((EXP_DEV, ff, share), BF16),
        in_specs=[fixed] * 5,
        out_specs=pl.BlockSpec(memory_space=pl.ANY),
        scratch_shapes=[
            pltpu.SMEM((block_slot.shape[1],), jnp.int32),
            pltpu.SMEM(block_count.shape, jnp.int32),
            pltpu.SMEM(replica_expert.shape, jnp.int32),
            pltpu.VMEM(hidden.shape, BF16),
            pltpu.VMEM(grad_out.shape, BF16),
            pltpu.VMEM((EXP_DEV, ff, share), BF16),
            pltpu.VMEM((2, (EXP_DEV + 1) * SUPER, hidden.shape[0]), BF16),
            pltpu.VMEM((4, EXP_DEV, ff, share), F32),
            pltpu.VMEM(column, BF16),
            pltpu.VMEM(column, BF16),
            pltpu.VMEM(column, BF16),
            pltpu.VMEM(column, BF16),
            pltpu.VMEM(column, BF16),
            pltpu.VMEM((4, EXP_DEV, ff, share), BF16),
            pltpu.VMEM((5, EXP_DEV, ff, share), BF16),
            pltpu.VMEM(early, BF16),
            pltpu.VMEM(early, BF16),
            dma((3,)), dma((6,)), dma, dma, dma, dma, dma,
            dma((chunks, 4)), dma((chunks, 4)), dma((chunks, 4)), dma((chunks, 5)),
            dma((max(EARLY, 1),)),
        ],
        compiler_params=pltpu.CompilerParams(
            collective_id=0, has_side_effects=True, vmem_limit_bytes=52 * 1024 * 1024
        ),
    )(
        pltpu.with_memory_space_constraint(block_slot[0], pltpu.HBM), block_count,
        pltpu.with_memory_space_constraint(replica_expert, pltpu.HBM), hidden, grad_out,
    )


def solution(mesh):
    in_specs = (
        P(("dp", "expert"), None),
        P(("dp", "expert"), None),
        P(("dp", "expert"), None),
        P(("dp", "expert")),
        P(),
    )
    out_specs = P("expert", None, "dp")
    return jax.shard_map(body, mesh=mesh, in_specs=in_specs, out_specs=out_specs, check_vma=False)
```
